32 devices in a mesh: groups: 2 (over x), lon: 16 (over z, y, core).
Axes of the slice: x: 2, y: 2, z: 4, core: 2. Of those that a mesh axis runs over, the one named last changes fastest.
Arguments:
- queries: bfloat16 [32, 128, 2560], P('groups', 'lon'), parts along dimension 0, may hold values from -6 to 6
- keys_values: bfloat16 [2, 32, 128, 2560], P(None, 'groups', 'lon'), parts along dimension 1, may hold values from -6 to 6
- out_weight: bfloat16 [2560, 2560], replicated, may hold values from -0.47851562 to 0.47851562
- reg_queries: bfloat16 [128, 2560], P('groups'), parts along dimension 0, may hold values from -6 to 6
Outputs:
- attn_out: bfloat16 [32, 128, 2560], P('groups', 'lon'), parts along dimension 0
- reg_out: bfloat16 [128, 2560], P('groups'), parts along dimension 0
The draws below stay inside these ranges and needn't reach their ends.
There are 2 independent parts, one for each index of `groups`. The reference program is written for one: setup_inputs(seed, part) draws one part's arguments, and reference() takes and returns one part's arrays. A program takes and returns all parts, laid end to end along the dimension named above; an argument that names none is the same for every part. Nothing has to cross between parts.
All inputs are finite; a program needn't handle non-finite values.
Results may differ from the reference program's by a relative error of at most 0.0057.
Values may be sent and summed in bfloat16 or wider, within the bound.
No kernel may reach another device: no remote copies, remote signals or barrier semaphores. Data moves between devices by JAX's collectives and lax.ppermute only.
A program may use at most 256 MiB of HBM per device.

```python
import math
import jax
import jax.numpy as jnp
from jax import lax

HEADS = 20
HEAD_DIM = 128
WIN = 7
REG = 64
LAT = 16
D = 2560
LON = 128


def draw_queries(key, part):
    normal_part = jnp.clip(jax.random.normal(jax.random.fold_in(key, 11), (LAT, LON, D), jnp.float32), -5.0, 5.0)
    return normal_part.astype(jnp.bfloat16)


def draw_keys_values(key, part):
    keys = jnp.clip(jax.random.normal(jax.random.fold_in(key, 21), (LAT, LON, D), jnp.float32), -5.0, 5.0)
    values = jnp.clip(jax.random.normal(jax.random.fold_in(key, 22), (LAT, LON, D), jnp.float32), -3.0, 3.0)
    return jnp.stack([keys, values], axis=0).astype(jnp.bfloat16)


def draw_reg_queries(key, part):
    normal_part = jnp.clip(jax.random.normal(jax.random.fold_in(key, 31), (REG, D), jnp.float32), -5.0, 5.0)
    return normal_part.astype(jnp.bfloat16)


def bell_draw(own_key, shape, deviation, most, kind=jnp.bfloat16):
    array = jax.random.normal(own_key, shape, jnp.float32) * deviation
    return jnp.minimum(jnp.maximum(array, -most), most).astype(kind)


def setup_inputs(seed: int = 0, part: int = 0) -> dict:
    key_of = jax.random.split(jax.random.key(seed), 5)
    part_keys = jax.random.split(jax.random.fold_in(key_of[4], part), 5)
    return {
        "queries": draw_queries(jax.random.fold_in(jax.random.fold_in(key_of[4], part), 71), part),
        "keys_values": draw_keys_values(jax.random.fold_in(jax.random.fold_in(key_of[4], part), 71), part),
        "out_weight": bell_draw(key_of[2], (D, D), 0.08, 0.47851562),
        "reg_queries": draw_reg_queries(jax.random.fold_in(jax.random.fold_in(key_of[4], part), 71), part),
    }


def window_attend(queries, keys_values):
    latitudes, columns, model_width = queries.shape
    factor = 1.0 / math.sqrt(HEAD_DIM)
    radius = WIN // 2
    first_row = jnp.clip(jnp.arange(latitudes, dtype=jnp.int32) - radius, 0, latitudes - WIN).astype(jnp.int32)
    query_heads = queries.astype(jnp.float32).reshape(latitudes, columns, HEADS, HEAD_DIM)
    scores = []
    for row_step in range(WIN):
        banded = jnp.take(keys_values[0], (first_row + row_step).astype(jnp.int32), axis=0)
        for col_step in range(-radius, radius + 1):
            shifted = jnp.roll(banded, -col_step, axis=1).astype(jnp.float32)
            shifted = shifted.reshape(latitudes, columns, HEADS, HEAD_DIM)
            scores.append(lax.optimization_barrier(jnp.sum(query_heads * shifted, axis=-1)) * factor)
    stacked = jnp.stack(scores, axis=-1)
    maxima = lax.optimization_barrier(jnp.max(stacked, axis=-1, keepdims=True))
    expon = jnp.exp(stacked - maxima)
    weights = (expon / lax.optimization_barrier(jnp.sum(expon, axis=-1, keepdims=True))).astype(jnp.bfloat16)
    blended = jnp.zeros((latitudes, columns, HEADS, HEAD_DIM), jnp.float32)
    offset = 0
    for row_step in range(WIN):
        banded = jnp.take(keys_values[1], (first_row + row_step).astype(jnp.int32), axis=0)
        for col_step in range(-radius, radius + 1):
            values = jnp.roll(banded, -col_step, axis=1).astype(jnp.float32)
            values = values.reshape(latitudes, columns, HEADS, HEAD_DIM)
            blended = blended + weights[..., offset][..., None].astype(jnp.float32) * values
            offset = offset + 1
    return blended.reshape(latitudes, columns, model_width).astype(jnp.bfloat16)

def reference(queries, keys_values, out_weight, reg_queries):
    latitudes, columns, model_width = queries.shape
    blended = window_attend(queries, keys_values)
    attn_out = jnp.dot(blended.reshape(-1, model_width), out_weight, preferred_element_type=jnp.float32)
    attn_out = attn_out.reshape(latitudes, columns, model_width).astype(jnp.bfloat16)
    factor = 1.0 / math.sqrt(HEAD_DIM)
    keys = keys_values[0].astype(jnp.float32).reshape(-1, HEADS, HEAD_DIM)
    values = keys_values[1].astype(jnp.float32).reshape(-1, HEADS, HEAD_DIM)
    reg_heads = reg_queries.astype(jnp.float32).reshape(REG, HEADS, HEAD_DIM)
    reg_scores = jnp.einsum('rhd,thd->hrt', reg_heads, keys) * factor
    reg_peak = lax.optimization_barrier(jnp.max(reg_scores, axis=-1))
    reg_exp = jnp.exp(reg_scores - reg_peak[..., None])
    reg_total = lax.optimization_barrier(jnp.sum(reg_exp, axis=-1))
    reg_weights = reg_exp.astype(jnp.bfloat16).astype(jnp.float32)
    reg_sum = jnp.einsum('hrt,thd->rhd', reg_weights, values)
    attended = (reg_sum / jnp.transpose(reg_total)[:, :, None]).reshape(REG, model_width).astype(jnp.bfloat16)
    projected = jnp.dot(attended, out_weight, preferred_element_type=jnp.float32)
    reg_out = projected * lax.rsqrt(lax.optimization_barrier(jnp.mean(projected * projected, axis=-1, keepdims=True)) + 1e-06)
    return (attn_out, reg_out.astype(jnp.bfloat16))
```

```python
import functools
import math

import jax
import jax.numpy as jnp
from jax import lax
from jax.experimental import pallas as pl
from jax.experimental.pallas import tpu as pltpu
from jax.sharding import PartitionSpec as P

HEADS = 20
HEAD_DIM = 128
WIN = 7
RADIUS = WIN // 2
SCALE = math.log2(math.e) / math.sqrt(HEAD_DIM)
NEG = -1e30
GROUP = 32
CHUNKS = 4
MIB = 1 << 20


VMEM = pl.BlockSpec(memory_space=pltpu.VMEM)
SMEM = pl.BlockSpec(memory_space=pltpu.SMEM)


def call(body, outs, flops, moved, exps=0, scratch=(), limit=8, name=None):
    shapes = [jax.ShapeDtypeStruct(shape, dtype) for shape, dtype in outs]

    def run(*args):
        return pl.pallas_call(
            body,
            out_shape=shapes,
            in_specs=[SMEM] + [VMEM] * (len(args) - 1),
            out_specs=[VMEM] * len(shapes),
            scratch_shapes=list(scratch),
            compiler_params=pltpu.CompilerParams(vmem_limit_bytes=limit * MIB),
            cost_estimate=pl.CostEstimate(flops=flops, bytes_accessed=moved, transcendentals=exps),
            name=name,
        )(*args)

    return run


def iota(shape, dim):
    return lax.broadcasted_iota(jnp.int32, shape, dim)


def mm(a, b, dims=((1,), (0,))):
    return lax.dot_general(a, b, (dims, ((), ())), preferred_element_type=jnp.float32)


def pack_body(cols, place, kv, near, far):
    odd = place[0] % 2
    tokens = kv.shape[1]
    count = tokens // cols * RADIUS
    row, token = iota((count, tokens), 0), iota((count, tokens), 1)
    base = row // RADIUS * cols + row % RADIUS
    high = cols - RADIUS
    pick_near = (token == base + jnp.where(odd == 1, 0, high)).astype(jnp.bfloat16)
    pick_far = (token == base + jnp.where(odd == 1, high, 0)).astype(jnp.bfloat16)
    width = 512
    for part in range(2):
        for start in range(0, kv.shape[2], width):
            block = kv[part, :, start : start + width]
            near[part, :, start : start + width] = mm(pick_near, block).astype(jnp.bfloat16)
            far[part, :, start : start + width] = mm(pick_far, block).astype(jnp.bfloat16)


def reg_body(place, q, kv, keep, send):
    rows = q.shape[0]
    half = rows // 2
    bit = place[0] % 2
    lane = iota((rows, HEAD_DIM), 1)
    peaks = jnp.zeros((rows, HEAD_DIM), jnp.float32)
    totals = jnp.zeros((rows, HEAD_DIM), jnp.float32)

    sums = []
    for head in range(HEADS):
        at = slice(head * HEAD_DIM, (head + 1) * HEAD_DIM)
        scores = mm(q[:, at], kv[0, :, at], ((1,), (1,))) * SCALE
        peak = jnp.max(scores, axis=-1, keepdims=True).astype(jnp.bfloat16).astype(jnp.float32)
        weights = jnp.exp2(scores - peak)
        total = jnp.sum(weights, axis=-1, keepdims=True)
        sums.append(mm(weights.astype(jnp.bfloat16), kv[1, :, at]).astype(jnp.bfloat16))
        peaks = jnp.where(lane == head, peak, peaks)
        totals = jnp.where((lane == head + GROUP) | (lane == head + 2 * GROUP), total, totals)
    rounded = totals.astype(jnp.bfloat16).astype(jnp.float32)
    stats = jnp.where(lane < GROUP, peaks, jnp.where(lane < 2 * GROUP, rounded, totals - rounded))
    value = jnp.concatenate(sums + [stats.astype(jnp.bfloat16)], axis=1)

    @pl.when(bit == 0)
    def _():
        keep[...] = value[:half]
        send[...] = value[half:]

    @pl.when(bit == 1)
    def _():
        keep[...] = value[half:]
        send[...] = value[:half]


def merge_body(level, split, last, place, mine, other, *outs):
    rows = mine.shape[0]
    lane = iota((rows, HEAD_DIM), 1)
    base = HEADS * HEAD_DIM
    a = mine[:, base:].astype(jnp.float32)
    b = other[:, base:].astype(jnp.float32)
    peak = jnp.maximum(a, b)
    ea, eb = jnp.exp2(a - peak), jnp.exp2(b - peak)

    def total_of(x):
        return pltpu.roll(x, HEAD_DIM - GROUP, 1) + pltpu.roll(x, HEAD_DIM - 2 * GROUP, 1)

    total = total_of(a) * ea + total_of(b) * eb
    pieces = []
    for head in range(HEADS):
        at = slice(head * HEAD_DIM, (head + 1) * HEAD_DIM)
        x = mine[:, at].astype(jnp.float32) * ea[:, head : head + 1]
        x = x + other[:, at].astype(jnp.float32) * eb[:, head : head + 1]
        if last:
            x = x / total[:, head : head + 1]
        pieces.append(x.astype(jnp.bfloat16))
    if not last:
        total = jnp.where(lane < GROUP, total, 0.0)
        rounded = total.astype(jnp.bfloat16).astype(jnp.float32)
        stats = jnp.where(lane < GROUP, peak, 0.0)
        stats = stats + pltpu.roll(rounded, GROUP, 1) + pltpu.roll(total - rounded, 2 * GROUP, 1)
        pieces.append(stats.astype(jnp.bfloat16))
    value = jnp.concatenate(pieces, axis=1)
    if not split:
        outs[0][...] = value
        return
    keep, send = outs
    half = rows // 2
    bit = (place[0] // level) % 2

    @pl.when(bit == 0)
    def _():
        keep[...] = value[:half]
        send[...] = value[half:]

    @pl.when(bit == 1)
    def _():
        keep[...] = value[half:]
        send[...] = value[:half]


def attend_body(cols, first, count, place, q, kv, near, far, out):
    tokens = q.shape[0]
    rows = tokens // cols
    edge = rows * RADIUS
    keys = tokens + 2 * edge
    padded = -(-keys // 128) * 128
    odd = place[0] % 2
    shape = (tokens, padded)
    query, key = iota(shape, 0), iota(shape, 1)
    near_key, far_key = key - tokens, key - tokens - edge
    near_col = near_key % RADIUS + jnp.where(odd == 1, -RADIUS, cols)
    far_col = far_key % RADIUS + jnp.where(odd == 1, cols, -RADIUS)
    own = key < tokens
    mid = key < tokens + edge
    key_row = jnp.where(own, key // cols, jnp.where(mid, near_key // RADIUS, far_key // RADIUS))
    key_col = jnp.where(own, key % cols, jnp.where(mid, near_col, far_col))
    top = jnp.clip(query // cols - RADIUS, 0, rows - WIN)
    gap = key_col - query % cols
    inside = (key_row >= top) & (key_row < top + WIN) & (gap >= -RADIUS) & (gap <= RADIUS)
    bias = jnp.where(inside & (key < keys), 0.0, NEG)
    fill = jnp.zeros((padded - keys, HEAD_DIM), jnp.bfloat16)
    for index in range(count):
        head = first + index
        at = slice(head * HEAD_DIM, (head + 1) * HEAD_DIM)
        k = jnp.concatenate([kv[0, :, at], near[0, :, at], far[0, :, at], fill], axis=0)
        v = jnp.concatenate([kv[1, :, at], near[1, :, at], far[1, :, at], fill], axis=0)
        scores = mm(q[:, at], k, ((1,), (1,))) * SCALE + bias
        peak = jnp.max(scores, axis=-1, keepdims=True)
        weights = jnp.exp2(scores - peak)
        total = jnp.sum(weights, axis=-1, keepdims=True)
        blend = mm(weights.astype(jnp.bfloat16), v) / total
        out[:, index * HEAD_DIM : (index + 1) * HEAD_DIM] = blend.astype(jnp.bfloat16)


def project_body(place, reg, weight, *refs):
    blended, (out, reg_out), (x, projected) = refs[:-4], refs[-4:-2], refs[-2:]
    tokens = out.shape[0]
    width = weight.shape[0]
    start = 0
    for piece in blended:
        x[:tokens, start : start + piece.shape[1]] = piece[...]
        start += piece.shape[1]
    x[tokens:, :] = reg[...]
    block = 512
    square = jnp.zeros((reg.shape[0], 1), jnp.float32)
    for start in range(0, width, block):
        y = mm(x[...], weight[:, start : start + block])
        out[:, start : start + block] = y[:tokens].astype(jnp.bfloat16)
        r = y[tokens:]
        projected[:, start : start + block] = r
        square = square + jnp.sum(r * r, axis=-1, keepdims=True)
    scale = lax.rsqrt(square / width + 1e-06)
    reg_out[...] = (projected[...] * scale).astype(jnp.bfloat16)


def per_device(queries, keys_values, out_weight, reg_queries):
    latitudes, columns, model_width = queries.shape
    tokens = latitudes * columns
    bf16 = jnp.bfloat16
    size = lax.axis_size("lon")
    index = lax.axis_index("lon")
    place = jnp.reshape(index, (1,)).astype(jnp.int32)
    kv = keys_values.reshape(2, tokens, model_width)
    q = queries.reshape(tokens, model_width)
    edge = latitudes * RADIUS
    regs = reg_queries.shape[0]

    def exchange(x, pairs):
        return lax.ppermute(x, "lon", pairs)

    def flip(level):
        return [(i, i ^ level) for i in range(size)]

    pairs_far = [(i, (i + 1) % size if i % 2 else (i - 1) % size) for i in range(size)]

    near, far = call(
        functools.partial(pack_body, columns),
        [((2, edge, model_width), bf16)] * 2,
        flops=8 * edge * tokens * model_width,
        moved=kv.size * 2,
        name="pack",
    )(place, kv)
    far_in = exchange(far, pairs_far)
    near_in = exchange(near, flip(1))

    wide = model_width + HEAD_DIM
    keep, send = call(
        reg_body,
        [((regs // 2, wide), bf16)] * 2,
        flops=4 * regs * tokens * model_width,
        moved=kv.size * 2,
        exps=regs * tokens * HEADS,
        name="regs",
    )(place, reg_queries, kv)

    levels = []
    level = 1
    while level < size:
        levels.append(level)
        level *= 2
    halved = 2
    other = exchange(send, flip(1))
    for step, level in enumerate(levels):
        split = step + 1 < halved
        last = step + 1 == len(levels)
        rows = keep.shape[0]
        shape = (rows // 2 if split else rows, model_width if last else wide)
        outs = call(
            functools.partial(merge_body, 2 * level, split, last),
            [(shape, bf16)] * (2 if split else 1),
            flops=rows * wide * 3,
            moved=rows * wide * 6,
            name=f"merge{step}",
        )(place, keep, other)
        if not last:
            keep = outs[0]
            other = exchange(outs[-1], flip(2 * level))
    attended = outs[0]
    for level in levels[:halved][::-1]:
        bit = (index // level) % 2
        other = exchange(attended, flip(level))
        attended = jnp.where(
            bit == 0,
            jnp.concatenate([attended, other]),
            jnp.concatenate([other, attended]),
        )

    each = HEADS // CHUNKS
    blended = []
    for chunk in range(CHUNKS):
        (piece,) = call(
            functools.partial(attend_body, columns, chunk * each, each),
            [((tokens, each * HEAD_DIM), bf16)],
            flops=4 * tokens * 256 * each * HEAD_DIM,
            moved=tokens * each * HEAD_DIM * 12,
            exps=tokens * 256 * each,
            name=f"attend{chunk}",
        )(place, q, kv, near_in, far_in)
        blended.append(piece)

    attn_out, reg_out = call(
        project_body,
        [((tokens, model_width), bf16), ((regs, model_width), bf16)],
        flops=2 * (tokens + regs) * model_width * model_width,
        moved=2 * model_width * model_width,
        scratch=(
            pltpu.VMEM((tokens + regs, model_width), bf16),
            pltpu.VMEM((regs, model_width), jnp.float32),
        ),
        limit=16,
        name="project",
    )(place, attended, out_weight, *blended)
    return (attn_out.reshape(latitudes, columns, model_width), reg_out)


def solution(mesh):
    in_specs = (P("groups", "lon", None), P(None, "groups", "lon", None), P(), P("groups", None))
    out_specs = (P("groups", "lon", None), P("groups", None))
    return jax.shard_map(
        per_device, mesh=mesh, in_specs=in_specs, out_specs=out_specs, check_vma=False
    )
```

```python
import functools
import math

import jax
import jax.numpy as jnp
from jax import lax
from jax.experimental import pallas as pl
from jax.experimental.pallas import tpu as pltpu
from jax.sharding import PartitionSpec as P


HEADS = 20
HEAD_DIM = 128
WIN = 7
RADIUS = WIN // 2
SCALE = math.log2(math.e) / math.sqrt(HEAD_DIM)
NEG = -1e30
GROUP = 32
CHUNKS = 4
BATCH = 4
MIB = 1 << 20


VMEM = pl.BlockSpec(memory_space=pltpu.VMEM)
SMEM = pl.BlockSpec(memory_space=pltpu.SMEM)
HBM = pl.BlockSpec(memory_space=pltpu.HBM)


def call(body, outs, flops, moved, exps=0, scratch=(), limit=8, space=VMEM):
    shapes = [jax.ShapeDtypeStruct(shape, dtype) for shape, dtype in outs]

    def run(*args):
        return pl.pallas_call(
            body,
            out_shape=shapes,
            in_specs=[SMEM] + [space] * (len(args) - 1),
            out_specs=[VMEM] * len(shapes),
            scratch_shapes=list(scratch),
            compiler_params=pltpu.CompilerParams(vmem_limit_bytes=limit * MIB),
            cost_estimate=pl.CostEstimate(flops=flops, bytes_accessed=moved, transcendentals=exps),
        )(*args)

    return run


def iota(shape, dim):
    return lax.broadcasted_iota(jnp.int32, shape, dim)


def mm(a, b, dims=((1,), (0,))):
    return lax.dot_general(a, b, (dims, ((), ())), preferred_element_type=jnp.float32)


def first_body(cols, place, kv_hbm, q_hbm, r_hbm, kv, q, near, far, keep, send, r, sems):
    tokens, width = q_hbm.shape
    rows = r_hbm.shape[0]
    half = rows // 2
    steps = HEADS // BATCH
    block = BATCH * HEAD_DIM
    copies = [pltpu.make_async_copy(r_hbm, r, sems.at[steps])]
    copies += [
        pltpu.make_async_copy(
            kv_hbm.at[:, :, pl.ds(step * block, block)],
            kv.at[:, :, pl.ds(step * block, block)],
            sems.at[step],
        )
        for step in range(steps)
    ]
    copies.append(pltpu.make_async_copy(q_hbm, q, sems.at[steps + 1]))
    for copy in copies:
        copy.start()
    bit = place[0] % 2
    count = tokens // cols * RADIUS
    row, token = iota((count, tokens), 0), iota((count, tokens), 1)
    base = row // RADIUS * cols + row % RADIUS
    high = cols - RADIUS
    pick_near = (token == base + jnp.where(bit == 1, 0, high)).astype(jnp.bfloat16)
    pick_far = (token == base + jnp.where(bit == 1, high, 0)).astype(jnp.bfloat16)
    pick = jnp.concatenate([pick_near, pick_far], axis=0)
    lane = iota((rows, HEAD_DIM), 1)
    peaks = jnp.zeros((rows, HEAD_DIM), jnp.float32)
    totals = jnp.zeros((rows, HEAD_DIM), jnp.float32)

    def store(value, at):
        low, high = value[:half], value[half:]
        keep[:, at] = jnp.where(bit == 0, low, high)
        send[:, at] = jnp.where(bit == 0, high, low).astype(send.dtype)

    copies[0].wait()
    for step in range(steps):
        copies[step + 1].wait()
        heads = range(step * BATCH, (step + 1) * BATCH)
        at = [slice(head * HEAD_DIM, (head + 1) * HEAD_DIM) for head in heads]
        scores = [mm(r[:, x], kv[0, :, x], ((1,), (1,))) * SCALE for x in at]
        whole = slice(step * block, (step + 1) * block)
        for part in range(2):
            picked = mm(pick, kv[part, :, whole]).astype(jnp.bfloat16)
            near[part, :, whole] = picked[:count]
            far[part, :, whole] = picked[count:]
        tops = [jnp.max(x, axis=-1, keepdims=True) for x in scores]
        tops = [x.astype(jnp.bfloat16).astype(jnp.float32) for x in tops]
        weights = [jnp.exp2(x - top) for x, top in zip(scores, tops)]
        parts = [jnp.sum(x, axis=-1, keepdims=True) for x in weights]
        sums = [mm(x.astype(jnp.bfloat16), kv[1, :, y]) for x, y in zip(weights, at)]
        for head, top, part, value, x in zip(heads, tops, parts, sums, at):
            peaks = jnp.where(lane == head, top, peaks)
            totals = jnp.where((lane == head + GROUP) | (lane == head + 2 * GROUP), part, totals)
            store(value, x)
    rounded = totals.astype(jnp.bfloat16).astype(jnp.float32)
    stats = jnp.where(lane < GROUP, peaks, jnp.where(lane < 2 * GROUP, rounded, totals - rounded))
    store(stats, slice(width, width + HEAD_DIM))
    copies[-1].wait()


def merge_body(level, split, last, place, mine, other, *outs):
    rows = mine.shape[0]
    lane = iota((rows, HEAD_DIM), 1)
    base = HEADS * HEAD_DIM
    a = mine[:, base:].astype(jnp.float32)
    b = other[:, base:].astype(jnp.float32)
    peak = jnp.maximum(a, b)
    ea, eb = jnp.exp2(a - peak), jnp.exp2(b - peak)

    def total_of(x):
        return pltpu.roll(x, HEAD_DIM - GROUP, 1) + pltpu.roll(x, HEAD_DIM - 2 * GROUP, 1)

    total = total_of(a) * ea + total_of(b) * eb
    pieces = []
    for head in range(HEADS):
        at = slice(head * HEAD_DIM, (head + 1) * HEAD_DIM)
        x = mine[:, at].astype(jnp.float32) * ea[:, head : head + 1]
        x = x + other[:, at].astype(jnp.float32) * eb[:, head : head + 1]
        if last:
            x = x / total[:, head : head + 1]
        pieces.append(x)
    if not last:
        total = jnp.where(lane < GROUP, total, 0.0)
        rounded = total.astype(jnp.bfloat16).astype(jnp.float32)
        stats = jnp.where(lane < GROUP, peak, 0.0)
        stats = stats + pltpu.roll(rounded, GROUP, 1) + pltpu.roll(total - rounded, 2 * GROUP, 1)
        pieces.append(stats)
    value = jnp.concatenate(pieces, axis=1)
    if not split:
        outs[0][...] = value.astype(outs[0].dtype)
        return
    keep, send = outs
    half = rows // 2
    bit = (place[0] // level) % 2

    @pl.when(bit == 0)
    def _():
        keep[...] = value[:half]
        send[...] = value[half:].astype(send.dtype)

    @pl.when(bit == 1)
    def _():
        keep[...] = value[half:]
        send[...] = value[:half].astype(send.dtype)


def attend_body(cols, first, count, place, q, kv, near, far, out):
    tokens = q.shape[0]
    rows = tokens // cols
    edge = rows * RADIUS
    keys = tokens + 2 * edge
    padded = -(-keys // 128) * 128
    odd = place[0] % 2
    shape = (tokens, padded)
    query, key = iota(shape, 0), iota(shape, 1)
    near_key, far_key = key - tokens, key - tokens - edge
    near_col = near_key % RADIUS + jnp.where(odd == 1, -RADIUS, cols)
    far_col = far_key % RADIUS + jnp.where(odd == 1, cols, -RADIUS)
    own = key < tokens
    mid = key < tokens + edge
    key_row = jnp.where(own, key // cols, jnp.where(mid, near_key // RADIUS, far_key // RADIUS))
    key_col = jnp.where(own, key % cols, jnp.where(mid, near_col, far_col))
    top = jnp.clip(query // cols - RADIUS, 0, rows - WIN)
    gap = key_col - query % cols
    inside = (key_row >= top) & (key_row < top + WIN) & (gap >= -RADIUS) & (gap <= RADIUS)
    bias = jnp.where(inside & (key < keys), 0.0, NEG)
    fill = jnp.zeros((padded - keys, HEAD_DIM), jnp.bfloat16)
    for index in range(count):
        head = first + index
        at = slice(head * HEAD_DIM, (head + 1) * HEAD_DIM)
        k = jnp.concatenate([kv[0, :, at], near[0, :, at], far[0, :, at], fill], axis=0)
        v = jnp.concatenate([kv[1, :, at], near[1, :, at], far[1, :, at], fill], axis=0)
        scores = mm(q[:, at], k, ((1,), (1,))) * SCALE + bias
        peak = jnp.max(scores, axis=-1, keepdims=True)
        weights = jnp.exp2(scores - peak)
        total = jnp.sum(weights, axis=-1, keepdims=True)
        blend = mm(weights.astype(jnp.bfloat16), v) / total
        out[:, index * HEAD_DIM : (index + 1) * HEAD_DIM] = blend.astype(jnp.bfloat16)


def join(out, start, bit, mine, other):
    rows = mine.shape[0]
    low, high = mine[...], other[...]
    out[start : start + rows] = jnp.where(bit == 0, low, high)
    out[start + rows : start + 2 * rows] = jnp.where(bit == 0, high, low)


def join_body(level, place, mine, other, out):
    join(out, 0, (place[0] // level) % 2, mine, other)


def project_body(place, mine, other, weight, *refs):
    blended, (out, reg_out), (x, projected) = refs[:-4], refs[-4:-2], refs[-2:]
    tokens = out.shape[0]
    width = weight.shape[0]
    start = 0
    for piece in blended:
        x[:tokens, start : start + piece.shape[1]] = piece[...]
        start += piece.shape[1]
    join(x, tokens, place[0] % 2, mine, other)
    block = 512
    square = jnp.zeros((reg_out.shape[0], 1), jnp.float32)
    for start in range(0, width, block):
        y = mm(x[...], weight[:, start : start + block])
        out[:, start : start + block] = y[:tokens].astype(jnp.bfloat16)
        r = y[tokens:]
        projected[:, start : start + block] = r
        square = square + jnp.sum(r * r, axis=-1, keepdims=True)
    scale = lax.rsqrt(square / width + 1e-06)
    reg_out[...] = (projected[...] * scale).astype(jnp.bfloat16)


def body(queries, keys_values, out_weight, reg_queries):
    latitudes, columns, model_width = queries.shape
    tokens = latitudes * columns
    bf16 = jnp.bfloat16
    size = lax.axis_size("lon")
    index = lax.axis_index("lon")
    place = jnp.reshape(index, (1,)).astype(jnp.int32)
    kv = keys_values.reshape(2, tokens, model_width)
    q = queries.reshape(tokens, model_width)
    edge = latitudes * RADIUS
    regs = reg_queries.shape[0]

    def exchange(x, pairs):
        return lax.ppermute(x, "lon", pairs)

    def flip(level):
        return [(i, i ^ level) for i in range(size)]

    pairs_far = [(i, (i + 1) % size if i % 2 else (i - 1) % size) for i in range(size)]

    wide = model_width + HEAD_DIM
    hbm = [pltpu.with_memory_space_constraint(x, pltpu.HBM) for x in (kv, q, reg_queries)]
    kv, q, near, far, keep, send = call(
        functools.partial(first_body, columns),
        [(kv.shape, bf16), (q.shape, bf16)]
        + [((2, edge, model_width), bf16)] * 2
        + [((regs // 2, wide), jnp.float32), ((regs // 2, wide), bf16)],
        flops=8 * edge * tokens * model_width + 4 * regs * tokens * model_width,
        moved=kv.size * 2,
        exps=regs * tokens * HEADS,
        scratch=(
            pltpu.VMEM(reg_queries.shape, bf16),
            pltpu.SemaphoreType.DMA((HEADS // BATCH + 2,)),
        ),
        space=HBM,
    )(place, *hbm)
    far_in = exchange(far, pairs_far)
    near_in = exchange(near, flip(1))

    levels = []
    level = 1
    while level < size:
        levels.append(level)
        level *= 2
    if len(levels) > 2:
        levels.append(levels.pop(1))
    halved = min(2, len(levels) - 1)
    other = exchange(send, flip(1))
    for step, level in enumerate(levels):
        split = step + 1 < halved
        last = step + 1 == len(levels)
        after = 0 if last else levels[step + 1]
        rows = keep.shape[0]
        shape = (rows // 2 if split else rows, model_width if last else wide)
        outs = call(
            functools.partial(merge_body, after, split, last),
            [(shape, jnp.float32), (shape, bf16)] if split else [(shape, bf16)],
            flops=rows * wide * 3,
            moved=rows * wide * 6,
        )(place, keep, other)
        if not last:
            keep = outs[0]
            other = exchange(outs[-1], flip(after))
    attended = outs[0]
    for step in range(halved - 1, -1, -1):
        other = exchange(attended, flip(levels[step]))
        if step:
            (attended,) = call(
                functools.partial(join_body, levels[step]),
                [((2 * attended.shape[0], model_width), bf16)],
                flops=attended.size,
                moved=attended.size * 8,
            )(place, attended, other)

    each = HEADS // CHUNKS
    blended = []
    for chunk in range(CHUNKS):
        (piece,) = call(
            functools.partial(attend_body, columns, chunk * each, each),
            [((tokens, each * HEAD_DIM), bf16)],
            flops=4 * tokens * 256 * each * HEAD_DIM,
            moved=tokens * each * HEAD_DIM * 12,
            exps=tokens * 256 * each,
        )(place, q, kv, near_in, far_in)
        blended.append(piece)

    attn_out, reg_out = call(
        project_body,
        [((tokens, model_width), bf16), ((regs, model_width), bf16)],
        flops=2 * (tokens + regs) * model_width * model_width,
        moved=2 * model_width * model_width,
        scratch=(
            pltpu.VMEM((tokens + regs, model_width), bf16),
            pltpu.VMEM((regs, model_width), jnp.float32),
        ),
        limit=16,
    )(place, attended, other, out_weight, *blended)
    return (attn_out.reshape(latitudes, columns, model_width), reg_out)


def solution(mesh):
    in_specs = (P("groups", "lon", None), P(None, "groups", "lon", None), P(), P("groups", None))
    out_specs = (P("groups", "lon", None), P("groups", None))
    return jax.shard_map(body, mesh=mesh, in_specs=in_specs, out_specs=out_specs, check_vma=False)
```

```python
import functools
import math

import jax
import jax.numpy as jnp
from jax import lax
from jax.experimental import pallas as pl
from jax.experimental.pallas import tpu as pltpu
from jax.sharding import PartitionSpec as P


HEADS = 20
HEAD_DIM = 128
WIN = 7
RADIUS = WIN // 2
SCALE = math.log2(math.e) / math.sqrt(HEAD_DIM)
NEG = -1e30
GROUP = 32
CHUNKS = 1
BATCH = 10
ABATCH = 5
PIECES = 2
LOADS = 2
MIB = 1 << 20


VMEM = pl.BlockSpec(memory_space=pltpu.VMEM)
SMEM = pl.BlockSpec(memory_space=pltpu.SMEM)
HBM = pl.BlockSpec(memory_space=pltpu.HBM)


def call(body, outs, flops, moved, exps=0, scratch=(), limit=8, space=VMEM):
    shapes = [jax.ShapeDtypeStruct(shape, dtype) for shape, dtype in outs]

    def run(*args):
        return pl.pallas_call(
            body,
            out_shape=shapes,
            in_specs=[SMEM] + [space] * (len(args) - 1),
            out_specs=[VMEM] * len(shapes),
            scratch_shapes=list(scratch),
            compiler_params=pltpu.CompilerParams(vmem_limit_bytes=limit * MIB),
            cost_estimate=pl.CostEstimate(flops=flops, bytes_accessed=moved, transcendentals=exps),
        )(*args)

    return run


def iota(shape, dim):
    return lax.broadcasted_iota(jnp.int32, shape, dim)


def mm(a, b, dims=((1,), (0,))):
    return lax.dot_general(a, b, (dims, ((), ())), preferred_element_type=jnp.float32)


def place_of(part, start, width):
    span = width * 2 // PIECES
    return part * (PIECES // 2) + start // span, start % span


def spread(far, part, start, value):
    for low in range(0, value.shape[1], HEAD_DIM):
        piece, at = place_of(part, start + low, HEADS * HEAD_DIM)
        far[piece][:, at : at + HEAD_DIM] = value[:, low : low + HEAD_DIM]


def first_body(cols, place, kv_hbm, r_hbm, kv, near, keep, send, *refs):
    far, (r, sems) = refs[:-2], refs[-2:]
    tokens, width = kv_hbm.shape[1:]
    rows = r_hbm.shape[0]
    half = rows // 2
    steps = HEADS // BATCH
    block = BATCH * HEAD_DIM
    copies = [pltpu.make_async_copy(r_hbm, r, sems.at[steps])]
    copies += [
        pltpu.make_async_copy(
            kv_hbm.at[:, :, pl.ds(step * block, block)],
            kv.at[:, :, pl.ds(step * block, block)],
            sems.at[step],
        )
        for step in range(steps)
    ]
    for copy in copies:
        copy.start()
    bit = place[0] % 2
    count = tokens // cols * RADIUS
    row, token = iota((count, tokens), 0), iota((count, tokens), 1)
    base = row // RADIUS * cols + row % RADIUS
    high = cols - RADIUS
    pick_near = (token == base + jnp.where(bit == 1, 0, high)).astype(jnp.bfloat16)
    pick_far = (token == base + jnp.where(bit == 1, high, 0)).astype(jnp.bfloat16)
    pick = jnp.concatenate([pick_near, pick_far], axis=0)
    lane = iota((rows, HEAD_DIM), 1)
    peaks = jnp.zeros((rows, HEAD_DIM), jnp.float32)
    totals = jnp.zeros((rows, HEAD_DIM), jnp.float32)

    def store(value, at):
        low, high = value[:half], value[half:]
        keep[:, at] = jnp.where(bit == 0, low, high)
        send[:, at] = jnp.where(bit == 0, high, low).astype(send.dtype)

    copies[0].wait()
    for step in range(steps):
        copies[step + 1].wait()
        heads = range(step * BATCH, (step + 1) * BATCH)
        at = [slice(head * HEAD_DIM, (head + 1) * HEAD_DIM) for head in heads]
        scores = [mm(r[:, x], kv[0, :, x], ((1,), (1,))) * SCALE for x in at]
        whole = slice(step * block, (step + 1) * block)
        for part in range(2):
            picked = mm(pick, kv[part, :, whole]).astype(jnp.bfloat16)
            near[part, :, whole] = picked[:count]
            spread(far, part, step * block, picked[count:])
        tops = [jnp.max(x, axis=-1, keepdims=True) for x in scores]
        tops = [x.astype(jnp.bfloat16).astype(jnp.float32) for x in tops]
        weights = [jnp.exp2(x - top) for x, top in zip(scores, tops)]
        parts = [jnp.sum(x, axis=-1, keepdims=True) for x in weights]
        sums = [mm(x.astype(jnp.bfloat16), kv[1, :, y]) for x, y in zip(weights, at)]
        for head, top, part, value, x in zip(heads, tops, parts, sums, at):
            peaks = jnp.where(lane == head, top, peaks)
            totals = jnp.where((lane == head + GROUP) | (lane == head + 2 * GROUP), part, totals)
            store(value, x)
    rounded = totals.astype(jnp.bfloat16).astype(jnp.float32)
    stats = jnp.where(lane < GROUP, peaks, jnp.where(lane < 2 * GROUP, rounded, totals - rounded))
    store(stats, slice(width, width + HEAD_DIM))


def merge_body(level, split, last, place, mine, other, *outs):
    rows = mine.shape[0]
    lane = iota((rows, HEAD_DIM), 1)
    base = HEADS * HEAD_DIM
    a = mine[:, base:].astype(jnp.float32)
    b = other[:, base:].astype(jnp.float32)
    peak = jnp.maximum(a, b)
    ea, eb = jnp.exp2(a - peak), jnp.exp2(b - peak)

    def total_of(x):
        return pltpu.roll(x, HEAD_DIM - GROUP, 1) + pltpu.roll(x, HEAD_DIM - 2 * GROUP, 1)

    total = total_of(a) * ea + total_of(b) * eb
    pieces = []
    for head in range(HEADS):
        at = slice(head * HEAD_DIM, (head + 1) * HEAD_DIM)
        x = mine[:, at].astype(jnp.float32) * ea[:, head : head + 1]
        x = x + other[:, at].astype(jnp.float32) * eb[:, head : head + 1]
        if last:
            x = x / total[:, head : head + 1]
        pieces.append(x)
    if not last:
        total = jnp.where(lane < GROUP, total, 0.0)
        rounded = total.astype(jnp.bfloat16).astype(jnp.float32)
        stats = jnp.where(lane < GROUP, peak, 0.0)
        stats = stats + pltpu.roll(rounded, GROUP, 1) + pltpu.roll(total - rounded, 2 * GROUP, 1)
        pieces.append(stats)
    value = jnp.concatenate(pieces, axis=1)
    if not split:
        outs[0][...] = value.astype(outs[0].dtype)
        return
    keep, send = outs
    half = rows // 2
    bit = (place[0] // level) % 2

    @pl.when(bit == 0)
    def _():
        keep[...] = value[:half]
        send[...] = value[half:].astype(send.dtype)

    @pl.when(bit == 1)
    def _():
        keep[...] = value[half:]
        send[...] = value[:half].astype(send.dtype)


def attend_body(cols, first, count, place, q, kv, near, *refs):
    far, out = refs[:-1], refs[-1]
    tokens = q.shape[0]
    rows = tokens // cols
    edge = rows * RADIUS
    keys = tokens + 2 * edge
    padded = -(-keys // 128) * 128
    odd = place[0] % 2
    shape = (tokens, padded)
    query, key = iota(shape, 0), iota(shape, 1)
    near_key, far_key = key - tokens, key - tokens - edge
    near_col = near_key % RADIUS + jnp.where(odd == 1, -RADIUS, cols)
    far_col = far_key % RADIUS + jnp.where(odd == 1, cols, -RADIUS)
    own = key < tokens
    mid = key < tokens + edge
    key_row = jnp.where(own, key // cols, jnp.where(mid, near_key // RADIUS, far_key // RADIUS))
    key_col = jnp.where(own, key % cols, jnp.where(mid, near_col, far_col))
    top = jnp.clip(query // cols - RADIUS, 0, rows - WIN)
    gap = key_col - query % cols
    inside = (key_row >= top) & (key_row < top + WIN) & (gap >= -RADIUS) & (gap <= RADIUS)
    bias = jnp.where(inside & (key < keys), 0.0, NEG)
    fill = jnp.zeros((padded - keys, HEAD_DIM), jnp.bfloat16)

    def keys_of(part, at):
        piece, start = place_of(part, at.start, kv.shape[2])
        side = far[piece][:, start : start + HEAD_DIM]
        return jnp.concatenate([kv[part, :, at], near[part, :, at], side, fill], axis=0)

    for low in range(0, count, ABATCH):
        span = range(low, min(low + ABATCH, count))
        ats = [slice((first + i) * HEAD_DIM, (first + i + 1) * HEAD_DIM) for i in span]
        scores = [mm(q[:, at], keys_of(0, at), ((1,), (1,))) for at in ats]
        scores = [x * SCALE + bias for x in scores]
        peaks = [jnp.max(x, axis=-1, keepdims=True) for x in scores]
        weights = [jnp.exp2(x - peak) for x, peak in zip(scores, peaks)]
        totals = [jnp.sum(x, axis=-1, keepdims=True) for x in weights]
        sums = [mm(x.astype(jnp.bfloat16), keys_of(1, at)) for x, at in zip(weights, ats)]
        for i, x, total in zip(span, sums, totals):
            out[:, i * HEAD_DIM : (i + 1) * HEAD_DIM] = (x / total).astype(jnp.bfloat16)


def join(out, start, bit, mine, other):
    rows = mine.shape[0]
    low, high = mine[...], other[...]
    out[start : start + rows] = jnp.where(bit == 0, low, high)
    out[start + rows : start + 2 * rows] = jnp.where(bit == 0, high, low)


def join_body(level, place, mine, other, out):
    join(out, 0, (place[0] // level) % 2, mine, other)


def load_body(part, place, source, target, sem):
    columns = target.shape[1]
    copy = pltpu.make_async_copy(source.at[:, pl.ds(part * columns, columns)], target, sem)
    copy.start()
    copy.wait()


def project_body(place, mine, other, *refs):
    weights, blended = refs[:LOADS], refs[LOADS:-4]
    (out, reg_out), (x, projected) = refs[-4:-2], refs[-2:]
    tokens = out.shape[0]
    width = out.shape[1]
    start = 0
    for piece in blended:
        x[:tokens, start : start + piece.shape[1]] = piece[...]
        start += piece.shape[1]
    join(x, tokens, place[0] % 2, mine, other)
    span = weights[0].shape[1]
    block = math.gcd(span, 512)
    square = jnp.zeros((reg_out.shape[0], 1), jnp.float32)
    for start in range(0, width, block):
        low = start % span
        y = mm(x[...], weights[start // span][:, low : low + block])
        out[:, start : start + block] = y[:tokens].astype(jnp.bfloat16)
        r = y[tokens:]
        projected[:, start : start + block] = r
        square = square + jnp.sum(r * r, axis=-1, keepdims=True)
    scale = lax.rsqrt(square / width + 1e-06)
    reg_out[...] = (projected[...] * scale).astype(jnp.bfloat16)


def body(queries, keys_values, out_weight, reg_queries):
    latitudes, columns, model_width = queries.shape
    tokens = latitudes * columns
    bf16 = jnp.bfloat16
    size = lax.axis_size("lon")
    index = lax.axis_index("lon")
    place = jnp.reshape(index, (1,)).astype(jnp.int32)
    kv = keys_values.reshape(2, tokens, model_width)
    q = queries.reshape(tokens, model_width)
    edge = latitudes * RADIUS
    regs = reg_queries.shape[0]

    def exchange(x, pairs):
        return lax.ppermute(x, "lon", pairs)

    def flip(level):
        return [(i, i ^ level) for i in range(size)]

    pairs_far = [(i, (i + 1) % size if i % 2 else (i - 1) % size) for i in range(size)]

    wide = model_width + HEAD_DIM
    hbm = [pltpu.with_memory_space_constraint(x, pltpu.HBM) for x in (kv, reg_queries)]
    kv, near, keep, send, *far = call(
        functools.partial(first_body, columns),
        [(kv.shape, bf16), ((2, edge, model_width), bf16)]
        + [((regs // 2, wide), jnp.float32), ((regs // 2, wide), bf16)]
        + [((edge, 2 * model_width // PIECES), bf16)] * PIECES,
        flops=8 * edge * tokens * model_width + 4 * regs * tokens * model_width,
        moved=kv.size * 2,
        exps=regs * tokens * HEADS,
        scratch=(
            pltpu.VMEM(reg_queries.shape, bf16),
            pltpu.SemaphoreType.DMA((HEADS // BATCH + 1,)),
        ),
        space=HBM,
    )(place, *hbm)
    far_in = []
    for piece in range(PIECES):
        far_in.append(exchange(far[piece], pairs_far))
    near_in = exchange(near, flip(1))

    levels = []
    level = 1
    while level < size:
        levels.append(level)
        level *= 2
    if len(levels) > 2:
        levels.append(levels.pop(1))
    halved = min(2, len(levels) - 1)
    other = exchange(send, flip(1))
    for step, level in enumerate(levels):
        split = step + 1 < halved
        last = step + 1 == len(levels)
        after = 0 if last else levels[step + 1]
        rows = keep.shape[0]
        shape = (rows // 2 if split else rows, model_width if last else wide)
        outs = call(
            functools.partial(merge_body, after, split, last),
            [(shape, jnp.float32), (shape, bf16)] if split else [(shape, bf16)],
            flops=rows * wide * 3,
            moved=rows * wide * 6,
        )(place, keep, other)
        if not last:
            keep = outs[0]
            other = exchange(outs[-1], flip(after))
    attended = outs[0]
    for step in range(halved - 1, -1, -1):
        other = exchange(attended, flip(levels[step]))
        if step:
            (attended,) = call(
                functools.partial(join_body, levels[step]),
                [((2 * attended.shape[0], model_width), bf16)],
                flops=attended.size,
                moved=attended.size * 8,
            )(place, attended, other)

    each = HEADS // CHUNKS
    blended = []
    for chunk in range(CHUNKS):
        (piece,) = call(
            functools.partial(attend_body, columns, chunk * each, each),
            [((tokens, each * HEAD_DIM), bf16)],
            flops=4 * tokens * 256 * each * HEAD_DIM,
            moved=tokens * each * HEAD_DIM * 12,
            exps=tokens * 256 * each,
        )(place, q, kv, near_in, *far_in)
        blended.append(piece)

    weight_hbm = pltpu.with_memory_space_constraint(out_weight, pltpu.HBM)
    weights = []
    for part in range(LOADS):
        weights += call(
            functools.partial(load_body, part),
            [((model_width, model_width // LOADS), bf16)],
            flops=1,
            moved=4 * model_width * model_width // LOADS,
            scratch=(pltpu.SemaphoreType.DMA,),
            space=HBM,
        )(place, weight_hbm)

    attn_out, reg_out = call(
        project_body,
        [((tokens, model_width), bf16), ((regs, model_width), bf16)],
        flops=2 * (tokens + regs) * model_width * model_width,
        moved=2 * model_width * model_width,
        scratch=(
            pltpu.VMEM((tokens + regs, model_width), bf16),
            pltpu.VMEM((regs, model_width), jnp.float32),
        ),
        limit=16,
    )(place, attended, other, *weights, *blended)
    return (attn_out.reshape(latitudes, columns, model_width), reg_out)


def solution(mesh):
    in_specs = (P("groups", "lon", None), P(None, "groups", "lon", None), P(), P("groups", None))
    out_specs = (P("groups", "lon", None), P("groups", None))
    return jax.shard_map(body, mesh=mesh, in_specs=in_specs, out_specs=out_specs, check_vma=False)
```

```python
import functools
import math

import jax
import jax.numpy as jnp
from jax import lax
from jax.experimental import pallas as pl
from jax.experimental.pallas import tpu as pltpu
from jax.sharding import PartitionSpec as P


HEADS = 20
HEAD_DIM = 128
WIN = 7
RADIUS = WIN // 2
SCALE = math.log2(math.e) / math.sqrt(HEAD_DIM)
NEG = -1e30
GROUP = 32
CHUNKS = 4
BATCH = 10
ABATCH = 5
PIECES = 2
LOADS = ()
COUNT = max(1, len(LOADS))
MIB = 1 << 20


VMEM = pl.BlockSpec(memory_space=pltpu.VMEM)
SMEM = pl.BlockSpec(memory_space=pltpu.SMEM)
HBM = pl.BlockSpec(memory_space=pltpu.HBM)


def call(body, outs, flops, moved, exps=0, scratch=(), limit=8, space=VMEM):
    shapes = [jax.ShapeDtypeStruct(shape, dtype) for shape, dtype in outs]

    def run(*args):
        return pl.pallas_call(
            body,
            out_shape=shapes,
            in_specs=[SMEM] + [space] * (len(args) - 1),
            out_specs=[VMEM] * len(shapes),
            scratch_shapes=list(scratch),
            compiler_params=pltpu.CompilerParams(vmem_limit_bytes=limit * MIB),
            cost_estimate=pl.CostEstimate(flops=flops, bytes_accessed=moved, transcendentals=exps),
        )(*args)

    return run


def iota(shape, dim):
    return lax.broadcasted_iota(jnp.int32, shape, dim)


def mm(a, b, dims=((1,), (0,))):
    return lax.dot_general(a, b, (dims, ((), ())), preferred_element_type=jnp.float32)


def place_of(part, start, width):
    span = width * 2 // PIECES
    return part * (PIECES // 2) + start // span, start % span


def spread(far, part, start, value):
    for low in range(0, value.shape[1], HEAD_DIM):
        piece, at = place_of(part, start + low, HEADS * HEAD_DIM)
        far[piece][:, at : at + HEAD_DIM] = value[:, low : low + HEAD_DIM]


def first_body(place, kv_hbm, r_hbm, kv, keep, send, r, sems):
    _, width = kv_hbm.shape[1:]
    rows = r_hbm.shape[0]
    half = rows // 2
    steps = HEADS // BATCH
    block = BATCH * HEAD_DIM
    copies = [pltpu.make_async_copy(r_hbm, r, sems.at[steps])]
    copies += [
        pltpu.make_async_copy(
            kv_hbm.at[:, :, pl.ds(step * block, block)],
            kv.at[:, :, pl.ds(step * block, block)],
            sems.at[step],
        )
        for step in range(steps)
    ]
    for copy in copies:
        copy.start()
    bit = place[0] % 2
    lane = iota((rows, HEAD_DIM), 1)
    peaks = jnp.zeros((rows, HEAD_DIM), jnp.float32)
    totals = jnp.zeros((rows, HEAD_DIM), jnp.float32)

    def store(value, at):
        low, high = value[:half], value[half:]
        keep[:, at] = jnp.where(bit == 0, low, high)
        send[:, at] = jnp.where(bit == 0, high, low).astype(send.dtype)

    copies[0].wait()
    for step in range(steps):
        copies[step + 1].wait()
        heads = range(step * BATCH, (step + 1) * BATCH)
        at = [slice(head * HEAD_DIM, (head + 1) * HEAD_DIM) for head in heads]
        scores = [mm(r[:, x], kv[0, :, x], ((1,), (1,))) * SCALE for x in at]
        tops = [jnp.max(x, axis=-1, keepdims=True) for x in scores]
        tops = [x.astype(jnp.bfloat16).astype(jnp.float32) for x in tops]
        weights = [jnp.exp2(x - top) for x, top in zip(scores, tops)]
        parts = [jnp.sum(x, axis=-1, keepdims=True) for x in weights]
        sums = [mm(x.astype(jnp.bfloat16), kv[1, :, y]) for x, y in zip(weights, at)]
        for head, top, part, value, x in zip(heads, tops, parts, sums, at):
            peaks = jnp.where(lane == head, top, peaks)
            totals = jnp.where((lane == head + GROUP) | (lane == head + 2 * GROUP), part, totals)
            store(value, x)
    rounded = totals.astype(jnp.bfloat16).astype(jnp.float32)
    stats = jnp.where(lane < GROUP, peaks, jnp.where(lane < 2 * GROUP, rounded, totals - rounded))
    store(stats, slice(width, width + HEAD_DIM))


def pack_body(cols, place, kv, near, *far):
    tokens, width = kv.shape[1:]
    bit = place[0] % 2
    count = tokens // cols * RADIUS
    row, token = iota((count, tokens), 0), iota((count, tokens), 1)
    base = row // RADIUS * cols + row % RADIUS
    high = cols - RADIUS
    pick_near = (token == base + jnp.where(bit == 1, 0, high)).astype(jnp.bfloat16)
    pick_far = (token == base + jnp.where(bit == 1, high, 0)).astype(jnp.bfloat16)
    pick = jnp.concatenate([pick_near, pick_far], axis=0)
    block = 512
    for start in range(0, width, block):
        whole = slice(start, start + block)
        for part in range(2):
            picked = mm(pick, kv[part, :, whole]).astype(jnp.bfloat16)
            near[part, :, whole] = picked[:count]
            spread(far, part, start, picked[count:])


def merge_body(level, split, last, place, mine, other, *outs):
    rows = mine.shape[0]
    lane = iota((rows, HEAD_DIM), 1)
    base = HEADS * HEAD_DIM
    a = mine[:, base:].astype(jnp.float32)
    b = other[:, base:].astype(jnp.float32)
    peak = jnp.maximum(a, b)
    ea, eb = jnp.exp2(a - peak), jnp.exp2(b - peak)

    def total_of(x):
        return pltpu.roll(x, HEAD_DIM - GROUP, 1) + pltpu.roll(x, HEAD_DIM - 2 * GROUP, 1)

    total = total_of(a) * ea + total_of(b) * eb
    pieces = []
    for head in range(HEADS):
        at = slice(head * HEAD_DIM, (head + 1) * HEAD_DIM)
        x = mine[:, at].astype(jnp.float32) * ea[:, head : head + 1]
        x = x + other[:, at].astype(jnp.float32) * eb[:, head : head + 1]
        if last:
            x = x / total[:, head : head + 1]
        pieces.append(x)
    if not last:
        total = jnp.where(lane < GROUP, total, 0.0)
        rounded = total.astype(jnp.bfloat16).astype(jnp.float32)
        stats = jnp.where(lane < GROUP, peak, 0.0)
        stats = stats + pltpu.roll(rounded, GROUP, 1) + pltpu.roll(total - rounded, 2 * GROUP, 1)
        pieces.append(stats)
    value = jnp.concatenate(pieces, axis=1)
    if not split:
        outs[0][...] = value.astype(outs[0].dtype)
        return
    keep, send = outs
    half = rows // 2
    bit = (place[0] // level) % 2

    @pl.when(bit == 0)
    def _():
        keep[...] = value[:half]
        send[...] = value[half:].astype(send.dtype)

    @pl.when(bit == 1)
    def _():
        keep[...] = value[half:]
        send[...] = value[:half].astype(send.dtype)


def attend_body(cols, first, count, place, q, kv, near, *refs):
    far, out = refs[:-1], refs[-1]
    tokens = q.shape[0]
    rows = tokens // cols
    edge = rows * RADIUS
    keys = tokens + 2 * edge
    padded = -(-keys // 128) * 128
    odd = place[0] % 2
    shape = (tokens, padded)
    query, key = iota(shape, 0), iota(shape, 1)
    near_key, far_key = key - tokens, key - tokens - edge
    near_col = near_key % RADIUS + jnp.where(odd == 1, -RADIUS, cols)
    far_col = far_key % RADIUS + jnp.where(odd == 1, cols, -RADIUS)
    own = key < tokens
    mid = key < tokens + edge
    key_row = jnp.where(own, key // cols, jnp.where(mid, near_key // RADIUS, far_key // RADIUS))
    key_col = jnp.where(own, key % cols, jnp.where(mid, near_col, far_col))
    top = jnp.clip(query // cols - RADIUS, 0, rows - WIN)
    gap = key_col - query % cols
    inside = (key_row >= top) & (key_row < top + WIN) & (gap >= -RADIUS) & (gap <= RADIUS)
    bias = jnp.where(inside & (key < keys), 0.0, NEG)
    fill = jnp.zeros((padded - keys, HEAD_DIM), jnp.bfloat16)

    def keys_of(part, at):
        piece, start = place_of(part, at.start, kv.shape[2])
        side = far[piece][:, start : start + HEAD_DIM]
        return jnp.concatenate([kv[part, :, at], near[part, :, at], side, fill], axis=0)

    for low in range(0, count, ABATCH):
        span = range(low, min(low + ABATCH, count))
        ats = [slice((first + i) * HEAD_DIM, (first + i + 1) * HEAD_DIM) for i in span]
        scores = [mm(q[:, at], keys_of(0, at), ((1,), (1,))) for at in ats]
        scores = [x * SCALE + bias for x in scores]
        peaks = [jnp.max(x, axis=-1, keepdims=True) for x in scores]
        weights = [jnp.exp2(x - peak) for x, peak in zip(scores, peaks)]
        totals = [jnp.sum(x, axis=-1, keepdims=True) for x in weights]
        sums = [mm(x.astype(jnp.bfloat16), keys_of(1, at)) for x, at in zip(weights, ats)]
        for i, x, total in zip(span, sums, totals):
            out[:, i * HEAD_DIM : (i + 1) * HEAD_DIM] = (x / total).astype(jnp.bfloat16)


def join(out, start, bit, mine, other):
    rows = mine.shape[0]
    low, high = mine[...], other[...]
    out[start : start + rows] = jnp.where(bit == 0, low, high)
    out[start + rows : start + 2 * rows] = jnp.where(bit == 0, high, low)


def join_body(level, place, mine, other, out):
    join(out, 0, (place[0] // level) % 2, mine, other)


def load_body(start, place, source, target, sem):
    columns = target.shape[1]
    copy = pltpu.make_async_copy(source.at[:, pl.ds(start, columns)], target, sem)
    copy.start()
    copy.wait()


def project_body(place, mine, other, *refs):
    weights, blended = refs[:COUNT], refs[COUNT:-4]
    (out, reg_out), (x, projected) = refs[-4:-2], refs[-2:]
    tokens = out.shape[0]
    width = out.shape[1]
    start = 0
    for piece in blended:
        x[:tokens, start : start + piece.shape[1]] = piece[...]
        start += piece.shape[1]
    join(x, tokens, place[0] % 2, mine, other)
    block = 512
    start = 0
    square = jnp.zeros((reg_out.shape[0], 1), jnp.float32)
    for weight in weights:
        for low in range(0, weight.shape[1], block):
            y = mm(x[...], weight[:, low : low + block])
            out[:, start : start + block] = y[:tokens].astype(jnp.bfloat16)
            r = y[tokens:]
            projected[:, start : start + block] = r
            square = square + jnp.sum(r * r, axis=-1, keepdims=True)
            start += block
    scale = lax.rsqrt(square / width + 1e-06)
    reg_out[...] = (projected[...] * scale).astype(jnp.bfloat16)


def body(queries, keys_values, out_weight, reg_queries):
    latitudes, columns, model_width = queries.shape
    tokens = latitudes * columns
    bf16 = jnp.bfloat16
    size = lax.axis_size("lon")
    index = lax.axis_index("lon")
    place = jnp.reshape(index, (1,)).astype(jnp.int32)
    kv = keys_values.reshape(2, tokens, model_width)
    q = queries.reshape(tokens, model_width)
    edge = latitudes * RADIUS
    regs = reg_queries.shape[0]

    def exchange(x, pairs):
        return lax.ppermute(x, "lon", pairs)

    def flip(level):
        return [(i, i ^ level) for i in range(size)]

    pairs_far = [(i, (i + 1) % size if i % 2 else (i - 1) % size) for i in range(size)]

    wide = model_width + HEAD_DIM
    hbm = [pltpu.with_memory_space_constraint(x, pltpu.HBM) for x in (kv, reg_queries)]
    kv, keep, send = call(
        first_body,
        [(kv.shape, bf16), ((regs // 2, wide), jnp.float32), ((regs // 2, wide), bf16)],
        flops=4 * regs * tokens * model_width,
        moved=kv.size * 2,
        exps=regs * tokens * HEADS,
        scratch=(
            pltpu.VMEM(reg_queries.shape, bf16),
            pltpu.SemaphoreType.DMA((HEADS // BATCH + 1,)),
        ),
        space=HBM,
    )(place, *hbm)
    near, *far = call(
        functools.partial(pack_body, columns),
        [((2, edge, model_width), bf16)] + [((edge, 2 * model_width // PIECES), bf16)] * PIECES,
        flops=8 * edge * tokens * model_width,
        moved=kv.size * 2,
    )(place, kv)
    far_in = []
    for piece in range(PIECES):
        far_in.append(exchange(far[piece], pairs_far))
    near_in = exchange(near, flip(1))

    levels = []
    level = 1
    while level < size:
        levels.append(level)
        level *= 2
    halved = min(2, len(levels) - 1)
    other = exchange(send, flip(1))
    for step, level in enumerate(levels):
        split = step + 1 < halved
        last = step + 1 == len(levels)
        after = 0 if last else levels[step + 1]
        rows = keep.shape[0]
        shape = (rows // 2 if split else rows, model_width if last else wide)
        outs = call(
            functools.partial(merge_body, after, split, last),
            [(shape, jnp.float32), (shape, bf16)] if split else [(shape, bf16)],
            flops=rows * wide * 3,
            moved=rows * wide * 6,
        )(place, keep, other)
        if not last:
            keep = outs[0]
            other = exchange(outs[-1], flip(after))
    attended = outs[0]
    for step in range(halved - 1, -1, -1):
        other = exchange(attended, flip(levels[step]))
        if step:
            (attended,) = call(
                functools.partial(join_body, levels[step]),
                [((2 * attended.shape[0], model_width), bf16)],
                flops=attended.size,
                moved=attended.size * 8,
            )(place, attended, other)

    each = HEADS // CHUNKS
    blended = []
    for chunk in range(CHUNKS):
        (piece,) = call(
            functools.partial(attend_body, columns, chunk * each, each),
            [((tokens, each * HEAD_DIM), bf16)],
            flops=4 * tokens * 256 * each * HEAD_DIM,
            moved=tokens * each * HEAD_DIM * 12,
            exps=tokens * 256 * each,
        )(place, q, kv, near_in, *far_in)
        blended.append(piece)

    weight_hbm = pltpu.with_memory_space_constraint(out_weight, pltpu.HBM)
    weights = [] if LOADS else [out_weight]
    for part, columns_here in enumerate(LOADS):
        weights += call(
            functools.partial(load_body, sum(LOADS[:part])),
            [((model_width, columns_here), bf16)],
            flops=1,
            moved=4 * model_width * columns_here,
            scratch=(pltpu.SemaphoreType.DMA,),
            space=HBM,
        )(place, weight_hbm)

    attn_out, reg_out = call(
        project_body,
        [((tokens, model_width), bf16), ((regs, model_width), bf16)],
        flops=2 * (tokens + regs) * model_width * model_width,
        moved=2 * model_width * model_width,
        scratch=(
            pltpu.VMEM((tokens + regs, model_width), bf16),
            pltpu.VMEM((regs, model_width), jnp.float32),
        ),
        limit=16,
    )(place, attended, other, *weights, *blended)
    return (attn_out.reshape(latitudes, columns, model_width), reg_out)


def solution(mesh):
    in_specs = (P("groups", "lon", None), P(None, "groups", "lon", None), P(), P("groups", None))
    out_specs = (P("groups", "lon", None), P("groups", None))
    return jax.shard_map(body, mesh=mesh, in_specs=in_specs, out_specs=out_specs, check_vma=False)
```

```python
import functools
import math

import jax
import jax.numpy as jnp
from jax import lax
from jax.experimental import pallas as pl
from jax.experimental.pallas import tpu as pltpu
from jax.sharding import PartitionSpec as P


HEADS = 20
HEAD_DIM = 128
WIN = 7
RADIUS = WIN // 2
SCALE = math.log2(math.e) / math.sqrt(HEAD_DIM)
NEG = -1e30
GROUP = 32
CHUNKS = 4
BATCH = HEADS
ABATCH = 5
PIECES = 2
LOADS = ()
COUNT = max(1, len(LOADS))
MIB = 1 << 20


VMEM = pl.BlockSpec(memory_space=pltpu.VMEM)
SMEM = pl.BlockSpec(memory_space=pltpu.SMEM)
HBM = pl.BlockSpec(memory_space=pltpu.HBM)


def call(body, outs, flops, moved, exps=0, scratch=(), limit=8, space=VMEM):
    shapes = [jax.ShapeDtypeStruct(shape, dtype) for shape, dtype in outs]

    def run(*args):
        return pl.pallas_call(
            body,
            out_shape=shapes,
            in_specs=[SMEM] + [space] * (len(args) - 1),
            out_specs=[VMEM] * len(shapes),
            scratch_shapes=list(scratch),
            compiler_params=pltpu.CompilerParams(vmem_limit_bytes=limit * MIB),
            cost_estimate=pl.CostEstimate(flops=flops, bytes_accessed=moved, transcendentals=exps),
        )(*args)

    return run


def iota(shape, dim):
    return lax.broadcasted_iota(jnp.int32, shape, dim)


def mm(a, b, dims=((1,), (0,))):
    return lax.dot_general(a, b, (dims, ((), ())), preferred_element_type=jnp.float32)


def place_of(part, start, width):
    span = width * 2 // PIECES
    return part * (PIECES // 2) + start // span, start % span


def spread(far, part, start, value):
    for low in range(0, value.shape[1], HEAD_DIM):
        piece, at = place_of(part, start + low, HEADS * HEAD_DIM)
        far[piece][:, at : at + HEAD_DIM] = value[:, low : low + HEAD_DIM]


def first_body(place, kv_hbm, r_hbm, kv, keep, send, r, sems):
    _, width = kv_hbm.shape[1:]
    rows = r_hbm.shape[0]
    half = rows // 2
    steps = HEADS // BATCH
    block = BATCH * HEAD_DIM
    copies = [pltpu.make_async_copy(r_hbm, r, sems.at[2 * steps])]
    copies += [
        pltpu.make_async_copy(
            kv_hbm.at[part, :, pl.ds(step * block, block)],
            kv.at[part, :, pl.ds(step * block, block)],
            sems.at[part * steps + step],
        )
        for part in range(2)
        for step in range(steps)
    ]
    for copy in copies:
        copy.start()
    bit = place[0] % 2
    lane = iota((rows, HEAD_DIM), 1)
    peaks = jnp.zeros((rows, HEAD_DIM), jnp.float32)
    totals = jnp.zeros((rows, HEAD_DIM), jnp.float32)

    def store(value, at):
        low, high = value[:half], value[half:]
        keep[:, at] = jnp.where(bit == 0, low, high)
        send[:, at] = jnp.where(bit == 0, high, low).astype(send.dtype)

    copies[0].wait()
    for step in range(steps):
        copies[step + 1].wait()
        heads = range(step * BATCH, (step + 1) * BATCH)
        at = [slice(head * HEAD_DIM, (head + 1) * HEAD_DIM) for head in heads]
        scores = [mm(r[:, x], kv[0, :, x], ((1,), (1,))) * SCALE for x in at]
        copies[steps + step + 1].wait()
        tops = [jnp.max(x, axis=-1, keepdims=True) for x in scores]
        tops = [x.astype(jnp.bfloat16).astype(jnp.float32) for x in tops]
        weights = [jnp.exp2(x - top) for x, top in zip(scores, tops)]
        parts = [jnp.sum(x, axis=-1, keepdims=True) for x in weights]
        sums = [mm(x.astype(jnp.bfloat16), kv[1, :, y]) for x, y in zip(weights, at)]
        for head, top, part, value, x in zip(heads, tops, parts, sums, at):
            peaks = jnp.where(lane == head, top, peaks)
            totals = jnp.where((lane == head + GROUP) | (lane == head + 2 * GROUP), part, totals)
            store(value, x)
    rounded = totals.astype(jnp.bfloat16).astype(jnp.float32)
    stats = jnp.where(lane < GROUP, peaks, jnp.where(lane < 2 * GROUP, rounded, totals - rounded))
    store(stats, slice(width, width + HEAD_DIM))


def pack_body(cols, place, kv, near, *far):
    tokens, width = kv.shape[1:]
    bit = place[0] % 2
    count = tokens // cols * RADIUS
    row, token = iota((count, tokens), 0), iota((count, tokens), 1)
    base = row // RADIUS * cols + row % RADIUS
    high = cols - RADIUS
    pick_near = (token == base + jnp.where(bit == 1, 0, high)).astype(jnp.bfloat16)
    pick_far = (token == base + jnp.where(bit == 1, high, 0)).astype(jnp.bfloat16)
    pick = jnp.concatenate([pick_near, pick_far], axis=0)
    block = 1280
    for start in range(0, width, block):
        whole = slice(start, start + block)
        for part in range(2):
            picked = mm(pick, kv[part, :, whole]).astype(jnp.bfloat16)
            near[part, :, whole] = picked[:count]
            spread(far, part, start, picked[count:])


def merge_body(level, split, last, place, mine, other, *outs):
    rows = mine.shape[0]
    lane = iota((rows, HEAD_DIM), 1)
    base = HEADS * HEAD_DIM
    a = mine[:, base:].astype(jnp.float32)
    b = other[:, base:].astype(jnp.float32)
    peak = jnp.maximum(a, b)
    ea, eb = jnp.exp2(a - peak), jnp.exp2(b - peak)

    def total_of(x):
        return pltpu.roll(x, HEAD_DIM - GROUP, 1) + pltpu.roll(x, HEAD_DIM - 2 * GROUP, 1)

    total = total_of(a) * ea + total_of(b) * eb
    pieces = []
    for head in range(HEADS):
        at = slice(head * HEAD_DIM, (head + 1) * HEAD_DIM)
        x = mine[:, at].astype(jnp.float32) * ea[:, head : head + 1]
        x = x + other[:, at].astype(jnp.float32) * eb[:, head : head + 1]
        if last:
            x = x / total[:, head : head + 1]
        pieces.append(x)
    if not last:
        total = jnp.where(lane < GROUP, total, 0.0)
        rounded = total.astype(jnp.bfloat16).astype(jnp.float32)
        stats = jnp.where(lane < GROUP, peak, 0.0)
        stats = stats + pltpu.roll(rounded, GROUP, 1) + pltpu.roll(total - rounded, 2 * GROUP, 1)
        pieces.append(stats)
    value = jnp.concatenate(pieces, axis=1)
    if not split:
        outs[0][...] = value.astype(outs[0].dtype)
        return
    keep, send = outs
    half = rows // 2
    bit = (place[0] // level) % 2

    @pl.when(bit == 0)
    def _():
        keep[...] = value[:half]
        send[...] = value[half:].astype(send.dtype)

    @pl.when(bit == 1)
    def _():
        keep[...] = value[half:]
        send[...] = value[:half].astype(send.dtype)


def attend_body(cols, first, count, place, q, kv, near, *refs):
    far, out = refs[:-1], refs[-1]
    tokens = q.shape[0]
    rows = tokens // cols
    edge = rows * RADIUS
    keys = tokens + 2 * edge
    padded = -(-keys // 128) * 128
    odd = place[0] % 2
    shape = (tokens, padded)
    query, key = iota(shape, 0), iota(shape, 1)
    near_key, far_key = key - tokens, key - tokens - edge
    near_col = near_key % RADIUS + jnp.where(odd == 1, -RADIUS, cols)
    far_col = far_key % RADIUS + jnp.where(odd == 1, cols, -RADIUS)
    own = key < tokens
    mid = key < tokens + edge
    key_row = jnp.where(own, key // cols, jnp.where(mid, near_key // RADIUS, far_key // RADIUS))
    key_col = jnp.where(own, key % cols, jnp.where(mid, near_col, far_col))
    top = jnp.clip(query // cols - RADIUS, 0, rows - WIN)
    gap = key_col - query % cols
    inside = (key_row >= top) & (key_row < top + WIN) & (gap >= -RADIUS) & (gap <= RADIUS)
    bias = jnp.where(inside & (key < keys), 0.0, NEG)
    fill = jnp.zeros((padded - keys, HEAD_DIM), jnp.bfloat16)

    def keys_of(part, at):
        piece, start = place_of(part, at.start, kv.shape[2])
        side = far[piece][:, start : start + HEAD_DIM]
        return jnp.concatenate([kv[part, :, at], near[part, :, at], side, fill], axis=0)

    for low in range(0, count, ABATCH):
        span = range(low, min(low + ABATCH, count))
        ats = [slice((first + i) * HEAD_DIM, (first + i + 1) * HEAD_DIM) for i in span]
        scores = [mm(q[:, at], keys_of(0, at), ((1,), (1,))) for at in ats]
        scores = [x * SCALE + bias for x in scores]
        peaks = [jnp.max(x, axis=-1, keepdims=True) for x in scores]
        weights = [jnp.exp2(x - peak) for x, peak in zip(scores, peaks)]
        totals = [jnp.sum(x, axis=-1, keepdims=True) for x in weights]
        sums = [mm(x.astype(jnp.bfloat16), keys_of(1, at)) for x, at in zip(weights, ats)]
        for i, x, total in zip(span, sums, totals):
            out[:, i * HEAD_DIM : (i + 1) * HEAD_DIM] = (x / total).astype(jnp.bfloat16)


def join(out, start, bit, mine, other):
    rows = mine.shape[0]
    low, high = mine[...], other[...]
    out[start : start + rows] = jnp.where(bit == 0, low, high)
    out[start + rows : start + 2 * rows] = jnp.where(bit == 0, high, low)


def join_body(level, place, mine, other, out):
    join(out, 0, (place[0] // level) % 2, mine, other)


def load_body(start, place, source, target, sem):
    columns = target.shape[1]
    copy = pltpu.make_async_copy(source.at[:, pl.ds(start, columns)], target, sem)
    copy.start()
    copy.wait()


def project_body(place, mine, other, *refs):
    weights, blended = refs[:COUNT], refs[COUNT:-4]
    (out, reg_out), (x, projected) = refs[-4:-2], refs[-2:]
    tokens = out.shape[0]
    width = out.shape[1]
    start = 0
    for piece in blended:
        x[:tokens, start : start + piece.shape[1]] = piece[...]
        start += piece.shape[1]
    join(x, tokens, place[0] % 2, mine, other)
    block = 256
    start = 0
    square = jnp.zeros((reg_out.shape[0], 1), jnp.float32)
    for weight in weights:
        for low in range(0, weight.shape[1], block):
            y = mm(x[...], weight[:, low : low + block])
            out[:, start : start + block] = y[:tokens].astype(jnp.bfloat16)
            r = y[tokens:]
            projected[:, start : start + block] = r
            square = square + jnp.sum(r * r, axis=-1, keepdims=True)
            start += block
    scale = lax.rsqrt(square / width + 1e-06)
    reg_out[...] = (projected[...] * scale).astype(jnp.bfloat16)


def body(queries, keys_values, out_weight, reg_queries):
    latitudes, columns, model_width = queries.shape
    tokens = latitudes * columns
    bf16 = jnp.bfloat16
    size = lax.axis_size("lon")
    index = lax.axis_index("lon")
    place = jnp.reshape(index, (1,)).astype(jnp.int32)
    kv = keys_values.reshape(2, tokens, model_width)
    q = queries.reshape(tokens, model_width)
    edge = latitudes * RADIUS
    regs = reg_queries.shape[0]

    def exchange(x, pairs):
        return lax.ppermute(x, "lon", pairs)

    def flip(level):
        return [(i, i ^ level) for i in range(size)]

    pairs_far = [(i, (i + 1) % size if i % 2 else (i - 1) % size) for i in range(size)]

    wide = model_width + HEAD_DIM
    hbm = [pltpu.with_memory_space_constraint(x, pltpu.HBM) for x in (kv, reg_queries)]
    kv, keep, send = call(
        first_body,
        [(kv.shape, bf16), ((regs // 2, wide), jnp.float32), ((regs // 2, wide), bf16)],
        flops=4 * regs * tokens * model_width,
        moved=kv.size * 2,
        exps=regs * tokens * HEADS,
        scratch=(
            pltpu.VMEM(reg_queries.shape, bf16),
            pltpu.SemaphoreType.DMA((2 * (HEADS // BATCH) + 1,)),
        ),
        space=HBM,
    )(place, *hbm)
    near, *far = call(
        functools.partial(pack_body, columns),
        [((2, edge, model_width), bf16)] + [((edge, 2 * model_width // PIECES), bf16)] * PIECES,
        flops=8 * edge * tokens * model_width,
        moved=kv.size * 2,
    )(place, kv)
    far_in = []
    for piece in range(PIECES):
        far_in.append(exchange(far[piece], pairs_far))
    near_in = exchange(near, flip(1))

    levels = []
    level = 1
    while level < size:
        levels.append(level)
        level *= 2
    halved = min(2, len(levels) - 1)
    other = exchange(send, flip(1))
    for step, level in enumerate(levels):
        split = step + 1 < halved
        last = step + 1 == len(levels)
        after = 0 if last else levels[step + 1]
        rows = keep.shape[0]
        shape = (rows // 2 if split else rows, model_width if last else wide)
        outs = call(
            functools.partial(merge_body, after, split, last),
            [(shape, jnp.float32), (shape, bf16)] if split else [(shape, bf16)],
            flops=rows * wide * 3,
            moved=rows * wide * 6,
        )(place, keep, other)
        if not last:
            keep = outs[0]
            other = exchange(outs[-1], flip(after))
    attended = outs[0]
    for step in range(halved - 1, -1, -1):
        other = exchange(attended, flip(levels[step]))
        if step:
            (attended,) = call(
                functools.partial(join_body, levels[step]),
                [((2 * attended.shape[0], model_width), bf16)],
                flops=attended.size,
                moved=attended.size * 8,
            )(place, attended, other)

    each = HEADS // CHUNKS
    blended = []
    for chunk in range(CHUNKS):
        (piece,) = call(
            functools.partial(attend_body, columns, chunk * each, each),
            [((tokens, each * HEAD_DIM), bf16)],
            flops=4 * tokens * 256 * each * HEAD_DIM,
            moved=tokens * each * HEAD_DIM * 12,
            exps=tokens * 256 * each,
        )(place, q, kv, near_in, *far_in)
        blended.append(piece)

    weight_hbm = pltpu.with_memory_space_constraint(out_weight, pltpu.HBM)
    weights = [] if LOADS else [out_weight]
    for part, columns_here in enumerate(LOADS):
        weights += call(
            functools.partial(load_body, sum(LOADS[:part])),
            [((model_width, columns_here), bf16)],
            flops=1,
            moved=4 * model_width * columns_here,
            scratch=(pltpu.SemaphoreType.DMA,),
            space=HBM,
        )(place, weight_hbm)

    attn_out, reg_out = call(
        project_body,
        [((tokens, model_width), bf16), ((regs, model_width), bf16)],
        flops=2 * (tokens + regs) * model_width * model_width,
        moved=2 * model_width * model_width,
        scratch=(
            pltpu.VMEM((tokens + regs, model_width), bf16),
            pltpu.VMEM((regs, model_width), jnp.float32),
        ),
        limit=16,
    )(place, attended, other, *weights, *blended)
    return (attn_out.reshape(latitudes, columns, model_width), reg_out)


def solution(mesh):
    in_specs = (P("groups", "lon", None), P(None, "groups", "lon", None), P(), P("groups", None))
    out_specs = (P("groups", "lon", None), P("groups", None))
    return jax.shard_map(body, mesh=mesh, in_specs=in_specs, out_specs=out_specs, check_vma=False)
```
